768 devices in a mesh: tm: 24 (over x_hi, z), height: 32 (over y, x_lo, core).
Axes of the slice: x: 4 (x_hi: 2, x_lo: 2; x = x_hi * 2 + x_lo), y: 8, z: 12, core: 2. Of those that a mesh axis runs over, the one named last changes fastest.
Arguments:
- query_tok: bfloat16 [24, 64, 64, 1536], P('tm', 'height'), may hold values from -6 to 6
- key_tok: bfloat16 [24, 64, 64, 1536], P('tm', 'height'), may hold values from -6 to 6
- value_tok: bfloat16 [24, 64, 64, 1536], P('tm', 'height'), may hold values from -6 to 6
- grad_out: bfloat16 [24, 64, 64, 1536], P('tm', 'height'), may hold values from -6 to 6
- far_picks: int32 [24, 32, 12, 2], P('tm', 'height'), may hold values from 0 to 3
Outputs:
- grad_query: bfloat16 [24, 64, 64, 1536], P('tm', 'height')
- grad_key: bfloat16 [24, 64, 64, 1536], P('tm', 'height')
- grad_value: bfloat16 [24, 64, 64, 1536], P('tm', 'height')
The draws below stay inside these ranges and needn't reach their ends.
All inputs are finite; a program needn't handle non-finite values.
Results may differ from the reference program's by a relative error of at most 0.012.
The reference program's roundings to bfloat16 on the way count: a program that leaves them out, or rounds other values in their place, can miss the bound.
Values may be sent and summed in bfloat16 or wider, within the bound.
A program may use at most 64 MiB of HBM per device.

```python
import jax
import jax.numpy as jnp
from jax import lax

HEADS = 12
HEAD_DIM = 128
FRAMES_DEV = 1
ROWS_DEV = 2
COLS = 64
REACH = 2
NPICK = 2
WIDTH = 1536
TILES_T = 24
TILES_H = 32
FRAMES = 24
ROWS = 64
TILE = 128
FACE = 64


def base_field(key):
    field = jax.random.truncated_normal(key, -6.0, 6.0, (FRAMES, ROWS, COLS, WIDTH), jnp.float32)
    return field.reshape(TILES_T, FRAMES_DEV, TILES_H, ROWS_DEV, COLS, WIDTH)


def draw_query_tok(key, part):
    field = base_field(jax.random.fold_in(key, 1))
    return field.reshape(FRAMES, ROWS, COLS, WIDTH).astype(jnp.bfloat16)


def draw_key_tok(key, part):
    field = base_field(jax.random.fold_in(key, 2))
    return field.reshape(FRAMES, ROWS, COLS, WIDTH).astype(jnp.bfloat16)


def place_ends(values, own_key, least, largest):
    shape = values.shape
    index_at = [jax.random.randint(jax.random.fold_in(own_key, axis), (), 0, shape[axis]) for axis in range(len(shape))]
    values = values.at[tuple(index_at)].set(least)
    longest = shape.index(max(shape))
    index_at[longest] = (index_at[longest] + 1) % shape[longest]
    return values.at[tuple(index_at)].set(largest)


def shard_levels(own_key, dims, pieces, low, high):
    loudness = 1.0
    for axis_at, parts in pieces:
        draws = jax.random.uniform(jax.random.fold_in(jax.random.fold_in(own_key, 6), axis_at), (parts,), jnp.float32, low / len(pieces), high / len(pieces))
        loudness = loudness * jnp.repeat(jnp.exp(draws), dims[axis_at] // parts).reshape((-1,) + (1,) * (len(dims) - 1 - axis_at))
    return loudness


def gaussian(stream_key, extent, deviation, reach, pieces=(), held_as=jnp.bfloat16):
    drawn = jax.random.normal(stream_key, extent, jnp.float32) * deviation
    if len(pieces) > 0:
        drawn = shard_levels(stream_key, extent, pieces, -0.22, 0.18) * drawn
    return jnp.clip(drawn, min=-reach, max=reach).astype(held_as)


def setup_inputs(seed: int = 0) -> dict:
    keys = jax.random.split(jax.random.key(seed), 6)
    return {
        "query_tok": draw_query_tok(jax.random.fold_in(keys[5], 71), 0),
        "key_tok": draw_key_tok(jax.random.fold_in(keys[5], 71), 0),
        "value_tok": gaussian(keys[2], (FRAMES, ROWS, COLS, WIDTH), 1.0, 6.0, ((0, 24), (1, 32))),
        "grad_out": gaussian(keys[3], (FRAMES, ROWS, COLS, WIDTH), 1.0, 6.0, ((0, 24), (1, 32))),
        "far_picks": place_ends(jax.random.randint(keys[4], (TILES_T, TILES_H, HEADS, NPICK), 0, 2 * REACH), jax.random.fold_in(keys[4], 1), 0, (2 * REACH) - 1).astype(jnp.int32),
    }


def pair_grads(query_rows, key_rows, value_rows, grad_rows, usable):
    score_scale = HEAD_DIM ** -0.5
    query_f = query_rows.astype(jnp.float32)
    key_f = key_rows.astype(jnp.float32)
    value_f = value_rows.astype(jnp.float32)
    grad_f = grad_rows.astype(jnp.float32)
    scores = jnp.einsum('qhd,khd->hqk', query_f, key_f) * score_scale
    scores = jnp.where(usable[:, None, :], scores, -jnp.inf)
    row_top = jnp.max(scores, axis=2, keepdims=True)
    expo = jnp.exp(scores - row_top)
    weights = expo / jnp.sum(expo, axis=2, keepdims=True)
    weights_b = weights.astype(jnp.bfloat16).astype(jnp.float32)
    attended = jnp.einsum('hqk,khd->qhd', weights_b, value_f)
    row_delta = jnp.sum(grad_f * attended, axis=2)
    value_grad = jnp.einsum('hqk,qhd->khd', weights_b, grad_f)
    grad_weights = jnp.einsum('qhd,khd->hqk', grad_f, value_f)
    dscore = (weights * (grad_weights - row_delta.T[:, :, None]) * score_scale).astype(jnp.bfloat16).astype(jnp.float32)
    query_grad = jnp.einsum('hqk,khd->qhd', dscore, key_f)
    key_grad = jnp.einsum('hqk,qhd->khd', dscore, query_f)
    return query_grad, key_grad, value_grad


def to_tiles(field):
    return field.reshape(TILES_T, FRAMES_DEV, TILES_H, ROWS_DEV, COLS, -1).transpose(0, 2, 1, 3, 4, 5)


def from_tiles(field):
    return field.transpose(0, 2, 1, 3, 4, 5).reshape(FRAMES, ROWS, COLS, -1)


def to_bf16_kept(field):
    rounded = field.astype(jnp.bfloat16)
    return lax.optimization_barrier(rounded).astype(jnp.float32)


def reference(query_tok, key_tok, value_tok, grad_out, far_picks):
    offset_list = [shift_by for shift_by in range(-REACH, REACH + 1) if shift_by != 0]
    offset_arr = jnp.array(offset_list, dtype=jnp.int32)
    query_t = to_tiles(query_tok)
    grad_t = to_tiles(grad_out)
    key_value = jnp.concatenate([to_tiles(key_tok), to_tiles(value_tok)], axis=-1)
    tile_pos = jnp.arange(TILES_H, dtype=jnp.int32)
    upper_ok = tile_pos > 0
    lower_ok = tile_pos < TILES_H - 1
    choose = jnp.arange(2 * REACH, dtype=jnp.int32)
    grads_fn = jax.vmap(pair_grads)

    def step(accum, frame_tile):
        own_tile = key_value[frame_tile]
        zero_face = jnp.zeros_like(own_tile[:1, :, ROWS_DEV - 1])
        upper = jnp.concatenate([zero_face, own_tile[:-1, :, ROWS_DEV - 1]], axis=0)
        lower = jnp.concatenate([own_tile[1:, :, 0], zero_face], axis=0)
        blocks = [own_tile.reshape(TILES_H, TILE, 2 * WIDTH), upper.reshape(TILES_H, FACE, 2 * WIDTH), lower.reshape(TILES_H, FACE, 2 * WIDTH)]
        for shift_by in offset_list:
            blocks.append(key_value[(frame_tile + shift_by) % TILES_T].reshape(TILES_H, TILE, 2 * WIDTH))
        stacked = jnp.concatenate(blocks, axis=1)
        total_keys = stacked.shape[1]
        target = frame_tile + offset_arr
        far_ok = (target >= 0) & (target < TILES_T)
        chosen = jnp.any(far_picks[frame_tile][..., None] == choose, axis=2) & far_ok[None, None, :]
        usable = jnp.concatenate([
            jnp.ones((TILES_H, HEADS, TILE), jnp.bool_),
            jnp.broadcast_to(upper_ok[:, None, None], (TILES_H, HEADS, FACE)),
            jnp.broadcast_to(lower_ok[:, None, None], (TILES_H, HEADS, FACE)),
            jnp.repeat(chosen, TILE, axis=2)], axis=2)
        query_grad, key_grad, value_grad = grads_fn(
            query_t[frame_tile].reshape(TILES_H, TILE, HEADS, HEAD_DIM),
            stacked[..., :WIDTH].reshape(TILES_H, total_keys, HEADS, HEAD_DIM),
            stacked[..., WIDTH:].reshape(TILES_H, total_keys, HEADS, HEAD_DIM),
            grad_t[frame_tile].reshape(TILES_H, TILE, HEADS, HEAD_DIM),
            usable)
        key_grads = jnp.concatenate([key_grad.reshape(TILES_H, total_keys, WIDTH), value_grad.reshape(TILES_H, total_keys, WIDTH)], axis=-1)
        own_part = key_grads[:, :TILE].reshape(TILES_H, FRAMES_DEV, ROWS_DEV, COLS, 2 * WIDTH)
        upper_grad = to_bf16_kept(key_grads[:, TILE:TILE + FACE].reshape(TILES_H, FRAMES_DEV, COLS, 2 * WIDTH))
        lower_grad = to_bf16_kept(key_grads[:, TILE + FACE:TILE + 2 * FACE].reshape(TILES_H, FRAMES_DEV, COLS, 2 * WIDTH))
        zero_grad = jnp.zeros_like(upper_grad[:1])
        into_last = jnp.concatenate([upper_grad[1:], zero_grad], axis=0)
        into_first = jnp.concatenate([zero_grad, lower_grad[:-1]], axis=0)
        own_part = own_part.at[:, :, ROWS_DEV - 1].add(into_last).at[:, :, 0].add(into_first)
        accum = accum.at[frame_tile].add(own_part)
        for slot_index, shift_by in enumerate(offset_list):
            start = TILE + 2 * FACE + slot_index * TILE
            rounded = to_bf16_kept(key_grads[:, start:start + TILE])
            accum = accum.at[(frame_tile + shift_by) % TILES_T].add(rounded.reshape(TILES_H, FRAMES_DEV, ROWS_DEV, COLS, 2 * WIDTH))
        return accum, query_grad.reshape(TILES_H, FRAMES_DEV, ROWS_DEV, COLS, WIDTH).astype(jnp.bfloat16)

    start_accum = jnp.zeros((TILES_T, TILES_H, FRAMES_DEV, ROWS_DEV, COLS, 2 * WIDTH), jnp.float32)
    accum, query_grads = lax.scan(step, start_accum, jnp.arange(TILES_T, dtype=jnp.int32))
    grad_query = from_tiles(query_grads)
    grad_key = from_tiles(accum[..., :WIDTH]).astype(jnp.bfloat16)
    grad_value = from_tiles(accum[..., WIDTH:]).astype(jnp.bfloat16)
    return (grad_query, grad_key, grad_value)
```

```python
import functools
import math

import jax
import jax.numpy as jnp
from jax import lax
from jax.experimental import pallas as pl
from jax.experimental.pallas import tpu as pltpu
from jax.sharding import PartitionSpec as P

HEAD_DIM = 128
MESH = pl.DeviceIdType.MESH
SCALE = HEAD_DIM ** -0.5
LOG2E = math.log2(math.e)
FAR = 1e30
REACHES = (-1, 1, -2, 2)
SLOTS = (1, 2, 0, 3)
NEAR_AT, LOCAL_AT, RELAY_AT, FAR_AT, MERGE_AT, GRAD_AT, PASS_AT, END_AT = 0, 6, 10, 13, 16, 18, 20, 22


def nt(a, b):
    return lax.dot_general(a, b, (((1,), (1,)), ((), ())), preferred_element_type=jnp.float32)


def nn(a, b):
    return lax.dot_general(a, b, (((1,), (0,)), ((), ())), preferred_element_type=jnp.float32)


def tn(a, b):
    return lax.dot_general(a, b, (((0,), (0,)), ((), ())), preferred_element_type=jnp.float32)


def flat(x):
    return x.reshape(x.shape[0] * x.shape[1], x.shape[2])


def kernel(
    sizes,
    picks, q_hbm, k_hbm, v_hbm, g_hbm,
    dq_out, dk_out, dv_out,
    qg, kv, far_qg, score, gradw, score0, gradw0,
    st_out, st_in, st_own, re_out, re_in,
    d2_out, d2_in, d1_part, d1_out, d1_in, dq_own, acc, face_out, face_in,
    load_sem, push_s, push_r, relay_s, relay_r, st_s, st_r, re_s, re_r,
    d2_s, d2_r, d1_s, d1_r, ff_s, ff_r, fb_s, fb_r,
):
    tiles_t, tiles_h, heads = sizes
    t = lax.axis_index("tm")
    h = lax.axis_index("height")
    there = [t >= 1, t <= tiles_t - 2, t >= 2, t <= tiles_t - 3]
    middle = (t >= 1) & (t <= tiles_t - 2)
    has_upper, has_lower = h >= 1, h <= tiles_h - 2
    face_there = [has_upper, has_lower]

    def tm_at(r):
        return {"tm": jnp.clip(t + r, 0, tiles_t - 1)}

    def height_at(r):
        return {"height": jnp.clip(h + r, 0, tiles_h - 1)}

    def remote(src, dst, send, recv, to):
        return pltpu.make_async_remote_copy(
            src_ref=src, dst_ref=dst, send_sem=send, recv_sem=recv, device_id=to, device_id_type=MESH
        )

    def loads(c):
        cols = pl.ds(pl.multiple_of(c * HEAD_DIM, HEAD_DIM), HEAD_DIM)
        return [
            pltpu.make_async_copy(q_hbm.at[0, :, :, cols], qg.at[c, 0], load_sem.at[0, c]),
            pltpu.make_async_copy(g_hbm.at[0, :, :, cols], qg.at[c, 1], load_sem.at[1, c]),
            pltpu.make_async_copy(k_hbm.at[0, :, :, cols], kv.at[c, 0, pl.ds(0, 2)], load_sem.at[2, c]),
            pltpu.make_async_copy(v_hbm.at[0, :, :, cols], kv.at[c, 1, pl.ds(0, 2)], load_sem.at[3, c]),
        ]

    def push(d, c):
        return remote(qg.at[c], far_qg.at[c, :, pl.ds(2 * d, 2)], push_s.at[d, c], push_r.at[d, c], tm_at(1 - 2 * d))

    def relay(d, c):
        return remote(
            far_qg.at[c, :, pl.ds(2 * d, 2)], far_qg.at[c, :, pl.ds(4 + 2 * d, 2)],
            relay_s.at[d, c], relay_r.at[d, c], tm_at(1 - 2 * d),
        )

    def stats(i, c):
        return remote(st_out.at[c, i], st_in.at[c, i ^ 1], st_s.at[i, c], st_r.at[i ^ 1, c], tm_at(REACHES[i]))

    def stats_got(i, c):
        return remote(st_out.at[c, i], st_in.at[c, i], st_s.at[i, c], st_r.at[i, c], tm_at(REACHES[i]))

    def ret(i, c):
        return remote(re_out.at[c, i], re_in.at[c, i ^ 1], re_s.at[i, c], re_r.at[i ^ 1, c], tm_at(REACHES[i]))

    def ret_got(i, c):
        return remote(re_out.at[c, i], re_in.at[c, i], re_s.at[i, c], re_r.at[i, c], tm_at(REACHES[i]))

    def dq2(d, c):
        return remote(d2_out.at[c, d], d2_in.at[c, d], d2_s.at[d, c], d2_r.at[d, c], tm_at(1 - 2 * d))

    def dq1(d, c):
        return remote(d1_out.at[c, d], d1_in.at[c, d], d1_s.at[d, c], d1_r.at[d, c], tm_at(1 - 2 * d))

    def face_push(e):
        return remote(kv.at[:, :, e], kv.at[:, :, 3 - e], ff_s.at[e], ff_r.at[1 - e], height_at(2 * e - 1))

    def face_got(e):
        return remote(kv.at[:, :, e], kv.at[:, :, 2 + e], ff_s.at[e], ff_r.at[e], height_at(2 * e - 1))

    def face_back(e, c):
        return remote(face_out.at[c, e], face_in.at[c, 1 - e], fb_s.at[e, c], fb_r.at[1 - e, c], height_at(2 * e - 1))

    def face_back_got(e, c):
        return remote(face_out.at[c, e], face_in.at[c, e], fb_s.at[e, c], fb_r.at[e, c], height_at(2 * e - 1))

    def each_head(body):
        def step(c, carry):
            body(c)
            return carry

        lax.fori_loop(0, heads, step, 0)

    @each_head
    def _(c):
        for copy in loads(c):
            copy.start()

    barrier = pltpu.get_barrier_semaphore()
    for r, ok in zip(REACHES, there):
        @pl.when(ok)
        def _():
            pl.semaphore_signal(barrier, inc=1, device_id=tm_at(r), device_id_type=MESH)
    for e in range(2):
        @pl.when(face_there[e])
        def _():
            pl.semaphore_signal(barrier, inc=1, device_id=height_at(2 * e - 1), device_id_type=MESH)

    for i in range(4):
        @pl.when(jnp.logical_not(there[i]))
        def _():
            far_qg[:, :, 2 * i : 2 * i + 2] = jnp.zeros((heads, 2, 2, 64, HEAD_DIM), jnp.bfloat16)
            st_in[:, i] = jnp.zeros((heads, 8, HEAD_DIM), jnp.float32)
            re_in[:, i] = jnp.zeros((heads, 8, HEAD_DIM), jnp.float32)
    for d in range(2):
        @pl.when(jnp.logical_not(middle))
        def _():
            d2_in[:, d] = jnp.zeros((heads, HEAD_DIM, HEAD_DIM), jnp.bfloat16)

        @pl.when(jnp.logical_not(there[d]))
        def _():
            d1_in[:, d] = jnp.zeros((heads, HEAD_DIM, HEAD_DIM), jnp.bfloat16)
    for e in range(2):
        @pl.when(jnp.logical_not(face_there[e]))
        def _():
            kv[:, :, 2 + e] = jnp.zeros((heads, 2, 64, HEAD_DIM), jnp.bfloat16)
            face_in[:, e] = jnp.zeros((heads, 2, 64, HEAD_DIM), jnp.bfloat16)

    pl.semaphore_wait(barrier, sum(ok.astype(jnp.int32) for ok in there + face_there))

    @each_head
    def _(c):
        q_load, g_load, k_load, v_load = loads(c)
        q_load.wait()
        g_load.wait()
        for d in range(2):
            @pl.when(there[1 - d])
            def _():
                push(d, c).start()

    @each_head
    def _(c):
        q_load, g_load, k_load, v_load = loads(c)
        k_load.wait()
        v_load.wait()

    for e in range(2):
        @pl.when(face_there[e])
        def _():
            face_push(e).start()

    def meet(c, first):
        rows = pl.ds(2 * first, 4)
        s = nt(flat(kv[c, 0, 0:2]), flat(far_qg[c, 0, rows])) * (SCALE * LOG2E)
        g = nt(flat(kv[c, 1, 0:2]), flat(far_qg[c, 1, rows]))
        cols = slice(first * HEAD_DIM, (first + 2) * HEAD_DIM)
        score[c, :, cols] = s
        gradw[c, :, cols] = g
        top = jnp.max(s, axis=0, keepdims=True)
        e = jnp.exp2(s - top)
        total = jnp.sum(e, axis=0, keepdims=True)
        delta = jnp.sum(e * g, axis=0, keepdims=True)
        for i in range(2):
            at = slice(i * HEAD_DIM, (i + 1) * HEAD_DIM)
            st_out[c, first + i, 0:1] = top[:, at]
            st_out[c, first + i, 1:2] = total[:, at]
            st_out[c, first + i, 2:3] = delta[:, at]

    def send_stats(c, first):
        for i in (first, first + 1):
            @pl.when(there[i])
            def _():
                stats(i, c).start()

    def stage(k, at, body):
        c = k - at

        @pl.when((c >= 0) & (c < heads))
        def _():
            body(c)

    def near(c):
        for d in range(2):
            @pl.when(there[d])
            def _():
                push(d, c).wait_recv()
        meet(c, 0)
        send_stats(c, 0)

    def send_on(c):
        for d in range(2):
            @pl.when(middle)
            def _():
                relay(d, c).start()

    def local(c):
        @pl.when(c == 0)
        def _():
            for e in range(2):
                @pl.when(face_there[e])
                def _():
                    face_got(e).wait_recv()

        s = nt(flat(kv[c, 0]), flat(qg[c, 0])) * (SCALE * LOG2E)
        g = nt(flat(kv[c, 1]), flat(qg[c, 1]))
        row = lax.broadcasted_iota(jnp.int32, s.shape, 0)
        upper_from = jnp.where(has_upper, 128, 192)
        lower_to = jnp.where(has_lower, 256, 192)
        usable = (row < 128) | ((row >= upper_from) & (row < lower_to))
        s = jnp.where(usable, s, -FAR)
        score0[c] = s
        gradw0[c] = g
        top = jnp.max(s, axis=0, keepdims=True)
        e = jnp.exp2(s - top)
        st_own[c, 0:1] = top
        st_own[c, 1:2] = jnp.sum(e, axis=0, keepdims=True)
        st_own[c, 2:3] = jnp.sum(e * g, axis=0, keepdims=True)

    def far(c):
        for d in range(2):
            @pl.when(there[2 + d])
            def _():
                relay(d, c).wait_recv()
        meet(c, 2)
        send_stats(c, 2)

    def merge(c):
        for i in range(4):
            @pl.when(there[i])
            def _():
                stats_got(i, c).wait_recv()
        off = []
        for i in range(4):
            chosen = ((picks[c, 0] == SLOTS[i]) | (picks[c, 1] == SLOTS[i])) & there[i]
            off.append(jnp.where(chosen, 0.0, FAR).astype(jnp.float32))
        tops = [st_own[c, 0:1]] + [st_in[c, i, 0:1] - off[i] for i in range(4)]
        totals = [st_own[c, 1:2]] + [st_in[c, i, 1:2] for i in range(4)]
        deltas = [st_own[c, 2:3]] + [st_in[c, i, 2:3] for i in range(4)]
        top = functools.reduce(jnp.maximum, tops)
        shares = [jnp.exp2(x - top) for x in tops]
        total = functools.reduce(jnp.add, [x * y for x, y in zip(totals, shares)])
        delta = functools.reduce(jnp.add, [x * y for x, y in zip(deltas, shares)]) / total
        lse = top + jnp.log(total) * LOG2E
        for i in range(4):
            re_out[c, i, 0:1] = lse + off[i]
            re_out[c, i, 1:2] = delta
        for i in range(4):
            @pl.when(there[i])
            def _():
                ret(i, c).start()
        w = jnp.exp2(score0[c] - lse)
        ds = (w * (gradw0[c] - delta) * SCALE).astype(jnp.bfloat16)
        value_part = nn(w.astype(jnp.bfloat16), flat(qg[c, 1]))
        key_part = nn(ds, flat(qg[c, 0]))
        dq_own[c] = tn(ds, flat(kv[c, 0]))
        acc[c, 0] = key_part[:128]
        acc[c, 1] = value_part[:128]
        for e in range(2):
            at = slice(128 + 64 * e, 192 + 64 * e)
            face_out[c, e, 0] = key_part[at].astype(jnp.bfloat16)
            face_out[c, e, 1] = value_part[at].astype(jnp.bfloat16)
        for e in range(2):
            @pl.when(face_there[e])
            def _():
                face_back(e, c).start()

    def grad(c):
        for i in range(4):
            @pl.when(there[i])
            def _():
                ret_got(i, c).wait_recv()
        ws, dss = [], []
        for i in range(4):
            at = slice(i * HEAD_DIM, (i + 1) * HEAD_DIM)
            w = jnp.exp2(score[c, :, at] - re_in[c, i, 0:1])
            ws.append(w.astype(jnp.bfloat16))
            dss.append((w * (gradw[c, :, at] - re_in[c, i, 1:2]) * SCALE).astype(jnp.bfloat16))
        w, ds = jnp.concatenate(ws, axis=1), jnp.concatenate(dss, axis=1)
        dq = tn(ds, flat(kv[c, 0, 0:2]))
        d1_part[c, 1] = dq[0:128]
        d1_part[c, 0] = dq[128:256]
        d2_out[c, 1] = dq[256:384].astype(jnp.bfloat16)
        d2_out[c, 0] = dq[384:512].astype(jnp.bfloat16)
        for d in range(2):
            @pl.when(there[3 - d])
            def _():
                dq2(d, c).start()
        acc[c, 0] += nn(ds, flat(far_qg[c, 0]))
        acc[c, 1] += nn(w, flat(far_qg[c, 1]))

    def pass_on(c):
        for d in range(2):
            @pl.when(middle)
            def _():
                dq2(d, c).wait_recv()
            d1_out[c, d] = (d1_part[c, d] + d2_in[c, d].astype(jnp.float32)).astype(jnp.bfloat16)

            @pl.when(there[1 - d])
            def _():
                dq1(d, c).start()

    def end(c):
        cols = pl.ds(pl.multiple_of(c * HEAD_DIM, HEAD_DIM), HEAD_DIM)
        for e in range(2):
            @pl.when(face_there[e])
            def _():
                face_back_got(e, c).wait_recv()
        for out, which in ((dk_out, 0), (dv_out, 1)):
            for e in range(2):
                part = acc[c, which, pl.ds(64 * e, 64)] + face_in[c, e, which].astype(jnp.float32)
                out[0, e, :, cols] = part.astype(jnp.bfloat16)
        for d in range(2):
            @pl.when(there[d])
            def _():
                dq1(d, c).wait_recv()
        dq = dq_own[c] + d1_in[c, 0].astype(jnp.float32) + d1_in[c, 1].astype(jnp.float32)
        dq_out[0, :, :, cols] = dq.astype(jnp.bfloat16).reshape(2, 64, HEAD_DIM)

    def tick(k, carry):
        stage(k, NEAR_AT, near)
        stage(k, RELAY_AT, send_on)
        stage(k, LOCAL_AT, local)
        stage(k, FAR_AT, far)
        stage(k, MERGE_AT, merge)
        stage(k, GRAD_AT, grad)
        stage(k, PASS_AT, pass_on)
        stage(k, END_AT, end)
        return carry

    lax.fori_loop(0, heads + END_AT, tick, 0)

    @each_head
    def _(c):
        for d in range(2):
            @pl.when(there[1 - d])
            def _():
                push(d, c).wait_send()
                dq1(d, c).wait_send()

            @pl.when(middle)
            def _():
                relay(d, c).wait_send()

            @pl.when(there[3 - d])
            def _():
                dq2(d, c).wait_send()

            @pl.when(face_there[d])
            def _():
                face_back(d, c).wait_send()
        for i in range(4):
            @pl.when(there[i])
            def _():
                stats(i, c).wait_send()
                ret(i, c).wait_send()

    for e in range(2):
        @pl.when(face_there[e])
        def _():
            face_push(e).wait_send()


def solution(mesh):
    tiles_t, tiles_h = mesh.shape["tm"], mesh.shape["height"]

    def per_device(query_tok, key_tok, value_tok, grad_out, far_picks):
        heads = query_tok.shape[3] // HEAD_DIM
        shape = query_tok.shape
        tile = HEAD_DIM
        bf, f32 = jnp.bfloat16, jnp.float32
        dma = pltpu.SemaphoreType.DMA
        any_spec = pl.BlockSpec(memory_space=pl.ANY)
        vmem_spec = pl.BlockSpec(memory_space=pltpu.VMEM)
        return pl.pallas_call(
            functools.partial(kernel, (tiles_t, tiles_h, heads)),
            out_shape=[jax.ShapeDtypeStruct(shape, bf)] * 3,
            in_specs=[pl.BlockSpec(memory_space=pltpu.SMEM)] + [any_spec] * 4,
            out_specs=[vmem_spec] * 3,
            scratch_shapes=[
                pltpu.VMEM((heads, 2, 2, 64, HEAD_DIM), bf),
                pltpu.VMEM((heads, 2, 4, 64, HEAD_DIM), bf),
                pltpu.VMEM((heads, 2, 8, 64, HEAD_DIM), bf),
                pltpu.VMEM((heads, tile, 4 * tile), f32),
                pltpu.VMEM((heads, tile, 4 * tile), f32),
                pltpu.VMEM((heads, 2 * tile, tile), f32),
                pltpu.VMEM((heads, 2 * tile, tile), f32),
                pltpu.VMEM((heads, 4, 8, tile), f32),
                pltpu.VMEM((heads, 4, 8, tile), f32),
                pltpu.VMEM((heads, 8, tile), f32),
                pltpu.VMEM((heads, 4, 8, tile), f32),
                pltpu.VMEM((heads, 4, 8, tile), f32),
                pltpu.VMEM((heads, 2, tile, HEAD_DIM), bf),
                pltpu.VMEM((heads, 2, tile, HEAD_DIM), bf),
                pltpu.VMEM((heads, 2, tile, HEAD_DIM), f32),
                pltpu.VMEM((heads, 2, tile, HEAD_DIM), bf),
                pltpu.VMEM((heads, 2, tile, HEAD_DIM), bf),
                pltpu.VMEM((heads, tile, HEAD_DIM), f32),
                pltpu.VMEM((heads, 2, tile, HEAD_DIM), f32),
                pltpu.VMEM((heads, 2, 2, 64, HEAD_DIM), bf),
                pltpu.VMEM((heads, 2, 2, 64, HEAD_DIM), bf),
                dma((4, heads)),
                dma((2, heads)), dma((2, heads)),
                dma((2, heads)), dma((2, heads)),
                dma((4, heads)), dma((4, heads)),
                dma((4, heads)), dma((4, heads)),
                dma((2, heads)), dma((2, heads)),
                dma((2, heads)), dma((2, heads)),
                dma((2,)), dma((2,)),
                dma((2, heads)), dma((2, heads)),
            ],
            compiler_params=pltpu.CompilerParams(
                collective_id=0, has_side_effects=True, vmem_limit_bytes=56 * 2**20
            ),
            name="tile_attention_grads",
        )(far_picks[0, 0], query_tok, key_tok, value_tok, grad_out)

    spec = P("tm", "height", None, None)
    return jax.shard_map(
        per_device, mesh=mesh, in_specs=(spec,) * 5, out_specs=(spec,) * 3, check_vma=False
    )
```

```python
import functools
import math

import jax
import jax.numpy as jnp
from jax import lax
from jax.experimental import pallas as pl
from jax.experimental.pallas import tpu as pltpu
from jax.sharding import PartitionSpec as P

HEAD_DIM = 128
MESH = pl.DeviceIdType.MESH
SCALE = HEAD_DIM ** -0.5
LOG2E = math.log2(math.e)
FAR = 1e30
REACHES = (-1, 1, -2, 2)
SLOTS = (1, 2, 0, 3)
NEAR_AT, LOCAL_AT, RELAY_AT, FAR_AT, MERGE_AT, GRAD_AT, PASS_AT, END_AT = 0, 18, 0, 12, 24, 32, 36, 40
FACES_AT = 4
LATER = 8


def nt(a, b):
    return lax.dot_general(a, b, (((1,), (1,)), ((), ())), preferred_element_type=jnp.float32)


def nn(a, b):
    return lax.dot_general(a, b, (((1,), (0,)), ((), ())), preferred_element_type=jnp.float32)


def tn(a, b):
    return lax.dot_general(a, b, (((0,), (0,)), ((), ())), preferred_element_type=jnp.float32)


def flat(x):
    return x.reshape(x.shape[0] * x.shape[1], x.shape[2])


def kernel(
    sizes,
    picks, q_hbm, k_hbm, v_hbm, g_hbm,
    dq_out, dk_out, dv_out,
    qg, kv, far_qg, score, gradw, score0, gradw0,
    st_out, st_in, st_own, re_out, re_in,
    d2_out, d2_in, d1_part, d1_out, d1_in, dq_own, acc, face_out, face_in, way_qg, way_dq, result,
    load_sem, push_s, push_r, relay_s, relay_r, st_s, st_r, re_s, re_r,
    d2_s, d2_r, d1_s, d1_r, ff_s, ff_r, fb_s, fb_r, way_s, way_r, ready, late, out_sem,
):
    tiles_t, tiles_h, heads = sizes
    t = lax.axis_index("tm")
    h = lax.axis_index("height")
    there = [t >= 1, t <= tiles_t - 2, t >= 2, t <= tiles_t - 3]
    middle = (t >= 1) & (t <= tiles_t - 2)
    has_upper, has_lower = h >= 1, h <= tiles_h - 2
    face_there = [has_upper, has_lower]
    low = tiles_t // 2 - 1
    crosses = [t == low, t == low + 1]
    ways = [tiles_t - 1, 0]
    finals = [low + 1, low]

    def tm_at(r):
        return {"tm": jnp.clip(t + r, 0, tiles_t - 1)}

    def height_at(r):
        return {"height": jnp.clip(h + r, 0, tiles_h - 1)}

    def remote(src, dst, send, recv, to):
        return pltpu.make_async_remote_copy(
            src_ref=src, dst_ref=dst, send_sem=send, recv_sem=recv, device_id=to, device_id_type=MESH
        )

    def loads(c):
        cols = pl.ds(pl.multiple_of(c * HEAD_DIM, HEAD_DIM), HEAD_DIM)
        return [
            pltpu.make_async_copy(q_hbm.at[0, :, :, cols], qg.at[c, 0], load_sem.at[0, c]),
            pltpu.make_async_copy(g_hbm.at[0, :, :, cols], qg.at[c, 1], load_sem.at[1, c]),
            pltpu.make_async_copy(k_hbm.at[0, :, :, cols], kv.at[c, 0, pl.ds(0, 2)], load_sem.at[2, c]),
            pltpu.make_async_copy(v_hbm.at[0, :, :, cols], kv.at[c, 1, pl.ds(0, 2)], load_sem.at[3, c]),
        ]

    def push(d, c):
        return remote(qg.at[c], far_qg.at[c, :, pl.ds(2 * d, 2)], push_s.at[d, c], push_r.at[d, c], tm_at(1 - 2 * d))

    def relay(d, c):
        return remote(
            far_qg.at[c, :, pl.ds(2 * d, 2)], far_qg.at[c, :, pl.ds(4 + 2 * d, 2)],
            relay_s.at[d, c], relay_r.at[d, c], tm_at(1 - 2 * d),
        )

    def stats(i, c):
        return remote(st_out.at[c, i], st_in.at[c, i ^ 1], st_s.at[i, c], st_r.at[i ^ 1, c], tm_at(REACHES[i]))

    def stats_got(i, c):
        return remote(st_out.at[c, i], st_in.at[c, i], st_s.at[i, c], st_r.at[i, c], tm_at(REACHES[i]))

    def ret(i, c):
        return remote(re_out.at[c, i], re_in.at[c, i ^ 1], re_s.at[i, c], re_r.at[i ^ 1, c], tm_at(REACHES[i]))

    def ret_got(i, c):
        return remote(re_out.at[c, i], re_in.at[c, i], re_s.at[i, c], re_r.at[i, c], tm_at(REACHES[i]))

    def dq2(d, c):
        return remote(d2_out.at[c, d], d2_in.at[c, d], d2_s.at[d, c], d2_r.at[d, c], tm_at(1 - 2 * d))

    def dq1(d, c):
        return remote(d1_out.at[c, d], d1_in.at[c, d], d1_s.at[d, c], d1_r.at[d, c], tm_at(1 - 2 * d))

    def start(copy, kind, d, c, src, sem):
        detour = crosses[d] & (lax.rem(c, 2) == 1)

        @pl.when(jnp.logical_not(detour))
        def _():
            copy(d, c).start()

        @pl.when(detour)
        def _():
            half = lax.div(c, 2)
            remote(src, way_at(kind, half), sem, way_r.at[kind, half], {"tm": ways[d]}).start()

    def way_at(kind, half):
        return way_qg.at[half, kind] if kind < 2 else way_dq.at[half, kind - 2]

    def forward(kind, d, c):
        half = lax.div(c, 2)
        dst, sem = (
            (far_qg.at[c, :, pl.ds(2 * d, 2)], push_r),
            (far_qg.at[c, :, pl.ds(4 + 2 * d, 2)], relay_r),
            (d2_in.at[c, d], d2_r),
            (d1_in.at[c, d], d1_r),
        )[kind]
        return remote(way_at(kind, half), dst, way_s.at[kind, half], sem.at[d, c], {"tm": finals[d]})

    def forward_got(kind, c):
        half = lax.div(c, 2)
        return remote(way_at(kind, half), way_at(kind, half), way_s.at[kind, half], way_r.at[kind, half], {"tm": finals[0]})

    def face_push(e):
        return remote(kv.at[:, :, e], kv.at[:, :, 3 - e], ff_s.at[e], ff_r.at[1 - e], height_at(2 * e - 1))

    def face_got(e):
        return remote(kv.at[:, :, e], kv.at[:, :, 2 + e], ff_s.at[e], ff_r.at[e], height_at(2 * e - 1))

    def face_back(e, c):
        return remote(face_out.at[c, e], face_in.at[c, 1 - e], fb_s.at[e, c], fb_r.at[1 - e, c], height_at(2 * e - 1))

    def face_back_got(e, c):
        return remote(face_out.at[c, e], face_in.at[c, e], fb_s.at[e, c], fb_r.at[e, c], height_at(2 * e - 1))

    def each_head(body):
        def step(c, carry):
            body(c)
            return carry

        lax.fori_loop(0, heads, step, 0)

    @each_head
    def _(c):
        for copy in loads(c):
            copy.start()

    barrier = pltpu.get_barrier_semaphore()
    for r, ok in zip(REACHES[:2], (there[0], there[1] & jnp.logical_not(crosses[0]))):
        @pl.when(ok)
        def _():
            pl.semaphore_signal(barrier, inc=1, device_id=tm_at(r), device_id_type=MESH)
    for e in range(2):
        @pl.when(face_there[e])
        def _():
            pl.semaphore_signal(barrier, inc=1, device_id=height_at(2 * e - 1), device_id_type=MESH)
    way = (t == ways[0]) | (t == ways[1])
    for at, to in ((ways[0], low), (ways[1], low), (ways[1], low + 1), (low + 1, ways[0])):
        @pl.when(t == at)
        def _():
            pl.semaphore_signal(barrier, inc=1, device_id={"tm": to}, device_id_type=MESH)

    for i in range(4):
        @pl.when(jnp.logical_not(there[i]))
        def _():
            far_qg[:, :, 2 * i : 2 * i + 2] = jnp.zeros((heads, 2, 2, 64, HEAD_DIM), jnp.bfloat16)
            st_in[:, i] = jnp.zeros((heads, 8, HEAD_DIM), jnp.float32)
            re_in[:, i] = jnp.zeros((heads, 8, HEAD_DIM), jnp.float32)
    for d in range(2):
        @pl.when(jnp.logical_not(middle))
        def _():
            d2_in[:, d] = jnp.zeros((heads, HEAD_DIM, HEAD_DIM), jnp.bfloat16)

        @pl.when(jnp.logical_not(there[d]))
        def _():
            d1_in[:, d] = jnp.zeros((heads, HEAD_DIM, HEAD_DIM), jnp.bfloat16)
    for e in range(2):
        @pl.when(jnp.logical_not(face_there[e]))
        def _():
            kv[:, :, 2 + e] = jnp.zeros((heads, 2, 64, HEAD_DIM), jnp.bfloat16)
            face_in[:, e] = jnp.zeros((heads, 2, 64, HEAD_DIM), jnp.bfloat16)

    peers = [there[0] & jnp.logical_not(crosses[1]), there[1], crosses[0], crosses[0], crosses[1], t == ways[0]]
    pl.semaphore_wait(barrier, sum(ok.astype(jnp.int32) for ok in peers + face_there))

    for r, ok in zip(REACHES[:2], there[:2]):
        @pl.when(ok & jnp.logical_not(crosses[1]))
        def _():
            pl.semaphore_signal(ready, inc=1, device_id=tm_at(r), device_id_type=MESH)
    for at in (ways[1], low + 1):
        @pl.when(crosses[0])
        def _():
            pl.semaphore_signal(late, inc=1, device_id={"tm": at}, device_id_type=MESH)

    @each_head
    def _(c):
        q_load, g_load, k_load, v_load = loads(c)
        k_load.wait()
        v_load.wait()

    def start_faces(ok):
        for e in range(2):
            @pl.when(face_there[e] & ok)
            def _():
                face_push(e).start()

    yields = crosses[0] | (t == ways[0])
    start_faces(jnp.logical_not(yields))

    @each_head
    def _(c):
        q_load, g_load, k_load, v_load = loads(c)
        q_load.wait()
        g_load.wait()

        @pl.when(there[1])
        def _():
            start(push, 0, 0, c, qg.at[c], push_s.at[0, c])

        @pl.when(there[0] & jnp.logical_not(crosses[1]))
        def _():
            start(push, 0, 1, c, qg.at[c], push_s.at[1, c])

    @pl.when(crosses[1])
    def _():
        pl.semaphore_wait(late, 1)
        for r in REACHES[:2]:
            pl.semaphore_signal(ready, inc=1, device_id=tm_at(r), device_id_type=MESH)

        @each_head
        def _(c):
            start(push, 0, 1, c, qg.at[c], push_s.at[1, c])

    def meet(c, first):
        rows = pl.ds(2 * first, 4)
        s = nt(flat(kv[c, 0, 0:2]), flat(far_qg[c, 0, rows])) * (SCALE * LOG2E)
        g = nt(flat(kv[c, 1, 0:2]), flat(far_qg[c, 1, rows]))
        cols = slice(first * HEAD_DIM, (first + 2) * HEAD_DIM)
        score[c, :, cols] = s
        gradw[c, :, cols] = g
        top = jnp.max(s, axis=0, keepdims=True)
        e = jnp.exp2(s - top)
        total = jnp.sum(e, axis=0, keepdims=True)
        delta = jnp.sum(e * g, axis=0, keepdims=True)
        for i in range(2):
            at = slice(i * HEAD_DIM, (i + 1) * HEAD_DIM)
            st_out[c, first + i, 0:1] = top[:, at]
            st_out[c, first + i, 1:2] = total[:, at]
            st_out[c, first + i, 2:3] = delta[:, at]

    def send_stats(c, first):
        for i in (first, first + 1):
            @pl.when(there[i])
            def _():
                stats(i, c).start()

    def stage(k, at, body):
        c = k - at

        @pl.when((c >= 0) & (c < heads))
        def _():
            body(c)

    def near(c):
        for d in range(2):
            @pl.when(there[d])
            def _():
                push(d, c).wait_recv()
        if RELAY_AT == NEAR_AT:
            send_on(c)
        meet(c, 0)
        send_stats(c, 0)

    def send_on(c):
        for d in range(2):
            @pl.when(middle)
            def _():
                start(relay, 1, d, c, far_qg.at[c, :, pl.ds(2 * d, 2)], relay_s.at[d, c])

    def local(c):
        @pl.when(c == 0)
        def _():
            for e in range(2):
                @pl.when(face_there[e])
                def _():
                    face_got(e).wait_recv()

        s = nt(flat(kv[c, 0]), flat(qg[c, 0])) * (SCALE * LOG2E)
        g = nt(flat(kv[c, 1]), flat(qg[c, 1]))
        row = lax.broadcasted_iota(jnp.int32, s.shape, 0)
        upper_from = jnp.where(has_upper, 128, 192)
        lower_to = jnp.where(has_lower, 256, 192)
        usable = (row < 128) | ((row >= upper_from) & (row < lower_to))
        s = jnp.where(usable, s, -FAR)
        score0[c] = s
        gradw0[c] = g
        top = jnp.max(s, axis=0, keepdims=True)
        e = jnp.exp2(s - top)
        st_own[c, 0:1] = top
        st_own[c, 1:2] = jnp.sum(e, axis=0, keepdims=True)
        st_own[c, 2:3] = jnp.sum(e * g, axis=0, keepdims=True)

    def far(c):
        @pl.when(c == 0)
        def _():
            pl.semaphore_wait(ready, sum(ok.astype(jnp.int32) for ok in there[:2]))

        for d in range(2):
            @pl.when(there[2 + d])
            def _():
                relay(d, c).wait_recv()
        meet(c, 2)
        send_stats(c, 2)

    def merge(c):
        for i in range(4):
            @pl.when(there[i])
            def _():
                stats_got(i, c).wait_recv()
        off = []
        for i in range(4):
            chosen = ((picks[c, 0] == SLOTS[i]) | (picks[c, 1] == SLOTS[i])) & there[i]
            off.append(jnp.where(chosen, 0.0, FAR).astype(jnp.float32))
        tops = [st_own[c, 0:1]] + [st_in[c, i, 0:1] - off[i] for i in range(4)]
        totals = [st_own[c, 1:2]] + [st_in[c, i, 1:2] for i in range(4)]
        deltas = [st_own[c, 2:3]] + [st_in[c, i, 2:3] for i in range(4)]
        top = functools.reduce(jnp.maximum, tops)
        shares = [jnp.exp2(x - top) for x in tops]
        total = functools.reduce(jnp.add, [x * y for x, y in zip(totals, shares)])
        delta = functools.reduce(jnp.add, [x * y for x, y in zip(deltas, shares)]) / total
        lse = top + jnp.log(total) * LOG2E
        for i in range(4):
            re_out[c, i, 0:1] = lse + off[i]
            re_out[c, i, 1:2] = delta
        for i in range(4):
            @pl.when(there[i])
            def _():
                ret(i, c).start()
        w = jnp.exp2(score0[c] - lse)
        ds = (w * (gradw0[c] - delta) * SCALE).astype(jnp.bfloat16)
        value_part = nn(w.astype(jnp.bfloat16), flat(qg[c, 1]))
        key_part = nn(ds, flat(qg[c, 0]))
        dq_own[c] = tn(ds, flat(kv[c, 0]))
        acc[c, 0] = key_part[:128]
        acc[c, 1] = value_part[:128]
        for e in range(2):
            at = slice(128 + 64 * e, 192 + 64 * e)
            face_out[c, e, 0] = key_part[at].astype(jnp.bfloat16)
            face_out[c, e, 1] = value_part[at].astype(jnp.bfloat16)
        for e in range(2):
            @pl.when(face_there[e])
            def _():
                face_back(e, c).start()

    def grad(c):
        for i in range(4):
            @pl.when(there[i])
            def _():
                ret_got(i, c).wait_recv()
        ws, dss = [], []
        for i in range(4):
            at = slice(i * HEAD_DIM, (i + 1) * HEAD_DIM)
            w = jnp.exp2(score[c, :, at] - re_in[c, i, 0:1])
            ws.append(w.astype(jnp.bfloat16))
            dss.append((w * (gradw[c, :, at] - re_in[c, i, 1:2]) * SCALE).astype(jnp.bfloat16))
        w, ds = jnp.concatenate(ws, axis=1), jnp.concatenate(dss, axis=1)
        dq = tn(ds, flat(kv[c, 0, 0:2]))
        d1_part[c, 1] = dq[0:128]
        d1_part[c, 0] = dq[128:256]
        d2_out[c, 1] = dq[256:384].astype(jnp.bfloat16)
        d2_out[c, 0] = dq[384:512].astype(jnp.bfloat16)
        for d in range(2):
            @pl.when(there[3 - d])
            def _():
                start(dq2, 2, d, c, d2_out.at[c, d], d2_s.at[d, c])
        acc[c, 0] += nn(ds, flat(far_qg[c, 0]))
        acc[c, 1] += nn(w, flat(far_qg[c, 1]))

    def pass_on(c):
        for d in range(2):
            @pl.when(middle)
            def _():
                dq2(d, c).wait_recv()
            d1_out[c, d] = (d1_part[c, d] + d2_in[c, d].astype(jnp.float32)).astype(jnp.bfloat16)

            @pl.when(there[1 - d])
            def _():
                start(dq1, 3, d, c, d1_out.at[c, d], d1_s.at[d, c])

    def store(o, c):
        cols = pl.ds(pl.multiple_of(c * HEAD_DIM, HEAD_DIM), HEAD_DIM)
        return pltpu.make_async_copy(
            result.at[c, o], (dq_out, dk_out, dv_out)[o].at[0, :, :, cols], out_sem.at[o, c]
        )

    def sent(c):
        for d in range(2):
            @pl.when(there[1 - d])
            def _():
                push(d, c).wait_send()

            @pl.when(middle)
            def _():
                relay(d, c).wait_send()

            @pl.when(there[3 - d])
            def _():
                dq2(d, c).wait_send()

            @pl.when(face_there[d])
            def _():
                face_back(d, c).wait_send()
        for i in range(4):
            @pl.when(there[i])
            def _():
                stats(i, c).wait_send()
                ret(i, c).wait_send()

    def end(c):
        sent(c)
        for e in range(2):
            @pl.when(face_there[e])
            def _():
                face_back_got(e, c).wait_recv()
        for which in range(2):
            for e in range(2):
                part = acc[c, which, pl.ds(64 * e, 64)] + face_in[c, e, which].astype(jnp.float32)
                result[c, 1 + which, e] = part.astype(jnp.bfloat16)
            store(1 + which, c).start()
        for d in range(2):
            @pl.when(there[d])
            def _():
                dq1(d, c).wait_recv()
        dq = dq_own[c] + d1_in[c, 0].astype(jnp.float32) + d1_in[c, 1].astype(jnp.float32)
        result[c, 0] = dq.astype(jnp.bfloat16).reshape(2, 64, HEAD_DIM)
        store(0, c).start()

    def on(kind, d):
        def body(c):
            @pl.when((t == ways[d]) & (lax.rem(c, 2) == 1))
            def _():
                if kind == 0 and d == 1:
                    @pl.when(c == 1)
                    def _():
                        pl.semaphore_wait(late, 1)
                forward_got(kind, c).wait_recv()
                forward(kind, d, c).start()

        return body

    def tick(k, carry):
        for kind, at in enumerate((NEAR_AT, FAR_AT - 1, PASS_AT - 1, END_AT - 1)):
            stage(k, at, on(kind, 0))
            stage(k, at + LATER, on(kind, 1))
        stage(k, NEAR_AT, near)

        @pl.when(k == FACES_AT)
        def _():
            start_faces(yields)

        if RELAY_AT != NEAR_AT:
            stage(k, RELAY_AT, send_on)
        stage(k, LOCAL_AT, local)
        stage(k, FAR_AT, far)
        stage(k, MERGE_AT, merge)
        stage(k, GRAD_AT, grad)
        stage(k, PASS_AT, pass_on)
        stage(k, END_AT, end)
        return carry

    lax.fori_loop(0, heads + END_AT + LATER, tick, 0)

    @each_head
    def _(c):
        for o in range(3):
            store(o, c).wait()
        for d in range(2):
            @pl.when(there[1 - d])
            def _():
                dq1(d, c).wait_send()

    @each_head
    def _(c):
        @pl.when(way & (lax.rem(c, 2) == 1))
        def _():
            for kind in range(4):
                forward(kind, 0, c).wait_send()

    for e in range(2):
        @pl.when(face_there[e])
        def _():
            face_push(e).wait_send()


def solution(mesh):
    tiles_t, tiles_h = mesh.shape["tm"], mesh.shape["height"]

    def per_device(query_tok, key_tok, value_tok, grad_out, far_picks):
        heads = query_tok.shape[3] // HEAD_DIM
        shape = query_tok.shape
        tile = HEAD_DIM
        bf, f32 = jnp.bfloat16, jnp.float32
        dma = pltpu.SemaphoreType.DMA
        any_spec = pl.BlockSpec(memory_space=pl.ANY)
        return pl.pallas_call(
            functools.partial(kernel, (tiles_t, tiles_h, heads)),
            out_shape=[jax.ShapeDtypeStruct(shape, bf)] * 3,
            in_specs=[pl.BlockSpec(memory_space=pltpu.SMEM)] + [any_spec] * 4,
            out_specs=[any_spec] * 3,
            scratch_shapes=[
                pltpu.VMEM((heads, 2, 2, 64, HEAD_DIM), bf),
                pltpu.VMEM((heads, 2, 4, 64, HEAD_DIM), bf),
                pltpu.VMEM((heads, 2, 8, 64, HEAD_DIM), bf),
                pltpu.VMEM((heads, tile, 4 * tile), f32),
                pltpu.VMEM((heads, tile, 4 * tile), f32),
                pltpu.VMEM((heads, 2 * tile, tile), f32),
                pltpu.VMEM((heads, 2 * tile, tile), f32),
                pltpu.VMEM((heads, 4, 8, tile), f32),
                pltpu.VMEM((heads, 4, 8, tile), f32),
                pltpu.VMEM((heads, 8, tile), f32),
                pltpu.VMEM((heads, 4, 8, tile), f32),
                pltpu.VMEM((heads, 4, 8, tile), f32),
                pltpu.VMEM((heads, 2, tile, HEAD_DIM), bf),
                pltpu.VMEM((heads, 2, tile, HEAD_DIM), bf),
                pltpu.VMEM((heads, 2, tile, HEAD_DIM), f32),
                pltpu.VMEM((heads, 2, tile, HEAD_DIM), bf),
                pltpu.VMEM((heads, 2, tile, HEAD_DIM), bf),
                pltpu.VMEM((heads, tile, HEAD_DIM), f32),
                pltpu.VMEM((heads, 2, tile, HEAD_DIM), f32),
                pltpu.VMEM((heads, 2, 2, 64, HEAD_DIM), bf),
                pltpu.VMEM((heads, 2, 2, 64, HEAD_DIM), bf),
                pltpu.VMEM((heads // 2, 2, 2, 2, 64, HEAD_DIM), bf),
                pltpu.VMEM((heads // 2, 2, tile, HEAD_DIM), bf),
                pltpu.VMEM((heads, 3, 2, 64, HEAD_DIM), bf),
                dma((4, heads)),
                dma((2, heads)), dma((2, heads)),
                dma((2, heads)), dma((2, heads)),
                dma((4, heads)), dma((4, heads)),
                dma((4, heads)), dma((4, heads)),
                dma((2, heads)), dma((2, heads)),
                dma((2, heads)), dma((2, heads)),
                dma((2,)), dma((2,)),
                dma((2, heads)), dma((2, heads)),
                dma((4, heads // 2)), dma((4, heads // 2)),
                pltpu.SemaphoreType.REGULAR, pltpu.SemaphoreType.REGULAR,
                dma((3, heads)),
            ],
            compiler_params=pltpu.CompilerParams(
                collective_id=0, has_side_effects=True, vmem_limit_bytes=56 * 2**20
            ),
            name="tile_attention_grads",
        )(far_picks[0, 0], query_tok, key_tok, value_tok, grad_out)

    spec = P("tm", "height", None, None)
    return jax.shard_map(
        per_device, mesh=mesh, in_specs=(spec,) * 5, out_specs=(spec,) * 3, check_vma=False
    )
```

```python
import functools
import math

import jax
import jax.numpy as jnp
from jax import lax
from jax.experimental import pallas as pl
from jax.experimental.pallas import tpu as pltpu
from jax.sharding import PartitionSpec as P

HEAD_DIM = 128
MESH = pl.DeviceIdType.MESH
SCALE = HEAD_DIM ** -0.5
LOG2E = math.log2(math.e)
FAR = 1e30
REACHES = (-1, 1, -2, 2)
SLOTS = (1, 2, 0, 3)
NEAR_AT, LOCAL_AT, RELAY_AT, FAR_AT, MERGE_AT, GRAD_AT, PASS_AT, END_AT = 0, 18, 0, 12, 24, 32, 36, 40
FACES_AT = 4
LATER = 8
WAY_KINDS, ON_AT = 2, 8


def nt(a, b):
    return lax.dot_general(a, b, (((1,), (1,)), ((), ())), preferred_element_type=jnp.float32)


def nn(a, b):
    return lax.dot_general(a, b, (((1,), (0,)), ((), ())), preferred_element_type=jnp.float32)


def tn(a, b):
    return lax.dot_general(a, b, (((0,), (0,)), ((), ())), preferred_element_type=jnp.float32)


def flat(x):
    return x.reshape(x.shape[0] * x.shape[1], x.shape[2])


def kernel(
    sizes,
    picks, q_hbm, k_hbm, v_hbm, g_hbm,
    dq_out, dk_out, dv_out,
    qg, kv, far_qg, score, gradw, score0, gradw0,
    st_out, st_in, st_own, re_out, re_in,
    d2_out, d2_in, d1_part, d1_out, d1_in, dq_own, acc, face_out, face_in, way_qg, way_dq, result,
    load_sem, push_s, push_r, relay_s, relay_r, st_s, st_r, re_s, re_r,
    d2_s, d2_r, d1_s, d1_r, ff_s, ff_r, fb_s, fb_r, way_s, way_r, ready, late, out_sem,
):
    tiles_t, tiles_h, heads = sizes
    t = lax.axis_index("tm")
    h = lax.axis_index("height")
    there = [t >= 1, t <= tiles_t - 2, t >= 2, t <= tiles_t - 3]
    middle = (t >= 1) & (t <= tiles_t - 2)
    has_upper, has_lower = h >= 1, h <= tiles_h - 2
    face_there = [has_upper, has_lower]
    low = tiles_t // 2 - 1
    crosses = [t == low, t == low + 1]
    ways = [tiles_t - 1, 0]
    finals = [low + 1, low]

    def tm_at(r):
        return {"tm": jnp.clip(t + r, 0, tiles_t - 1)}

    def height_at(r):
        return {"height": jnp.clip(h + r, 0, tiles_h - 1)}

    def remote(src, dst, send, recv, to):
        return pltpu.make_async_remote_copy(
            src_ref=src, dst_ref=dst, send_sem=send, recv_sem=recv, device_id=to, device_id_type=MESH
        )

    def loads(c):
        cols = pl.ds(pl.multiple_of(c * HEAD_DIM, HEAD_DIM), HEAD_DIM)
        return [
            pltpu.make_async_copy(q_hbm.at[0, :, :, cols], qg.at[c, 0], load_sem.at[0, c]),
            pltpu.make_async_copy(g_hbm.at[0, :, :, cols], qg.at[c, 1], load_sem.at[1, c]),
            pltpu.make_async_copy(k_hbm.at[0, :, :, cols], kv.at[c, 0, pl.ds(0, 2)], load_sem.at[2, c]),
            pltpu.make_async_copy(v_hbm.at[0, :, :, cols], kv.at[c, 1, pl.ds(0, 2)], load_sem.at[3, c]),
        ]

    def push(d, c):
        return remote(qg.at[c], far_qg.at[c, :, pl.ds(2 * d, 2)], push_s.at[d, c], push_r.at[d, c], tm_at(1 - 2 * d))

    def relay(d, c):
        return remote(
            far_qg.at[c, :, pl.ds(2 * d, 2)], far_qg.at[c, :, pl.ds(4 + 2 * d, 2)],
            relay_s.at[d, c], relay_r.at[d, c], tm_at(1 - 2 * d),
        )

    def stats(i, c):
        return remote(st_out.at[c, i], st_in.at[c, i ^ 1], st_s.at[i, c], st_r.at[i ^ 1, c], tm_at(REACHES[i]))

    def stats_got(i, c):
        return remote(st_out.at[c, i], st_in.at[c, i], st_s.at[i, c], st_r.at[i, c], tm_at(REACHES[i]))

    def ret(i, c):
        return remote(re_out.at[c, i], re_in.at[c, i ^ 1], re_s.at[i, c], re_r.at[i ^ 1, c], tm_at(REACHES[i]))

    def ret_got(i, c):
        return remote(re_out.at[c, i], re_in.at[c, i], re_s.at[i, c], re_r.at[i, c], tm_at(REACHES[i]))

    def dq2(d, c):
        return remote(d2_out.at[c, d], d2_in.at[c, d], d2_s.at[d, c], d2_r.at[d, c], tm_at(1 - 2 * d))

    def dq1(d, c):
        return remote(d1_out.at[c, d], d1_in.at[c, d], d1_s.at[d, c], d1_r.at[d, c], tm_at(1 - 2 * d))

    def start(copy, kind, d, c, src, sem):
        if kind >= WAY_KINDS:
            copy(d, c).start()
            return
        detour = crosses[d] & (lax.rem(c, 2) == 1)

        @pl.when(jnp.logical_not(detour))
        def _():
            copy(d, c).start()

        @pl.when(detour)
        def _():
            half = lax.div(c, 2)
            remote(src, way_at(kind, half), sem, way_r.at[kind, half], {"tm": ways[d]}).start()

    def way_at(kind, half):
        return way_qg.at[half, kind] if kind < 2 else way_dq.at[half, kind - 2]

    def forward(kind, d, c):
        half = lax.div(c, 2)
        dst, sem = (
            (far_qg.at[c, :, pl.ds(2 * d, 2)], push_r),
            (far_qg.at[c, :, pl.ds(4 + 2 * d, 2)], relay_r),
            (d2_in.at[c, d], d2_r),
            (d1_in.at[c, d], d1_r),
        )[kind]
        return remote(way_at(kind, half), dst, way_s.at[kind, half], sem.at[d, c], {"tm": finals[d]})

    def forward_got(kind, c):
        half = lax.div(c, 2)
        return remote(way_at(kind, half), way_at(kind, half), way_s.at[kind, half], way_r.at[kind, half], {"tm": finals[0]})

    def face_push(e):
        return remote(kv.at[:, :, e], kv.at[:, :, 3 - e], ff_s.at[e], ff_r.at[1 - e], height_at(2 * e - 1))

    def face_got(e):
        return remote(kv.at[:, :, e], kv.at[:, :, 2 + e], ff_s.at[e], ff_r.at[e], height_at(2 * e - 1))

    def face_back(e, c):
        return remote(face_out.at[c, e], face_in.at[c, 1 - e], fb_s.at[e, c], fb_r.at[1 - e, c], height_at(2 * e - 1))

    def face_back_got(e, c):
        return remote(face_out.at[c, e], face_in.at[c, e], fb_s.at[e, c], fb_r.at[e, c], height_at(2 * e - 1))

    def each_head(body):
        def step(c, carry):
            body(c)
            return carry

        lax.fori_loop(0, heads, step, 0)

    @each_head
    def _(c):
        for copy in loads(c):
            copy.start()

    barrier = pltpu.get_barrier_semaphore()
    for r, ok in zip(REACHES[:2], (there[0], there[1] & jnp.logical_not(crosses[0]))):
        @pl.when(ok)
        def _():
            pl.semaphore_signal(barrier, inc=1, device_id=tm_at(r), device_id_type=MESH)
    for e in range(2):
        @pl.when(face_there[e])
        def _():
            pl.semaphore_signal(barrier, inc=1, device_id=height_at(2 * e - 1), device_id_type=MESH)
    way = (t == ways[0]) | (t == ways[1])
    for at, to in ((ways[0], low), (ways[1], low), (ways[1], low + 1), (low + 1, ways[0])):
        @pl.when(t == at)
        def _():
            pl.semaphore_signal(barrier, inc=1, device_id={"tm": to}, device_id_type=MESH)

    for i in range(4):
        @pl.when(jnp.logical_not(there[i]))
        def _():
            far_qg[:, :, 2 * i : 2 * i + 2] = jnp.zeros((heads, 2, 2, 64, HEAD_DIM), jnp.bfloat16)
            st_in[:, i] = jnp.zeros((heads, 8, HEAD_DIM), jnp.float32)
            re_in[:, i] = jnp.zeros((heads, 8, HEAD_DIM), jnp.float32)
    for d in range(2):
        @pl.when(jnp.logical_not(middle))
        def _():
            d2_in[:, d] = jnp.zeros((heads, HEAD_DIM, HEAD_DIM), jnp.bfloat16)

        @pl.when(jnp.logical_not(there[d]))
        def _():
            d1_in[:, d] = jnp.zeros((heads, HEAD_DIM, HEAD_DIM), jnp.bfloat16)
    for e in range(2):
        @pl.when(jnp.logical_not(face_there[e]))
        def _():
            kv[:, :, 2 + e] = jnp.zeros((heads, 2, 64, HEAD_DIM), jnp.bfloat16)
            face_in[:, e] = jnp.zeros((heads, 2, 64, HEAD_DIM), jnp.bfloat16)

    peers = [there[0] & jnp.logical_not(crosses[1]), there[1], crosses[0], crosses[0], crosses[1], t == ways[0]]
    pl.semaphore_wait(barrier, sum(ok.astype(jnp.int32) for ok in peers + face_there))

    for r, ok in zip(REACHES[:2], there[:2]):
        @pl.when(ok & jnp.logical_not(crosses[1]))
        def _():
            pl.semaphore_signal(ready, inc=1, device_id=tm_at(r), device_id_type=MESH)
    for at in (ways[1], low + 1):
        @pl.when(crosses[0])
        def _():
            pl.semaphore_signal(late, inc=1, device_id={"tm": at}, device_id_type=MESH)

    @each_head
    def _(c):
        q_load, g_load, k_load, v_load = loads(c)
        k_load.wait()
        v_load.wait()

    def start_faces(ok):
        for e in range(2):
            @pl.when(face_there[e] & ok)
            def _():
                face_push(e).start()

    yields = crosses[0] | (t == ways[0])
    start_faces(jnp.logical_not(yields))

    @each_head
    def _(c):
        q_load, g_load, k_load, v_load = loads(c)
        q_load.wait()
        g_load.wait()

        @pl.when(there[1])
        def _():
            start(push, 0, 0, c, qg.at[c], push_s.at[0, c])

        @pl.when(there[0] & jnp.logical_not(crosses[1]))
        def _():
            start(push, 0, 1, c, qg.at[c], push_s.at[1, c])

    @pl.when(crosses[1])
    def _():
        pl.semaphore_wait(late, 1)
        for r in REACHES[:2]:
            pl.semaphore_signal(ready, inc=1, device_id=tm_at(r), device_id_type=MESH)

        @each_head
        def _(c):
            start(push, 0, 1, c, qg.at[c], push_s.at[1, c])

    def meet(c, first):
        rows = pl.ds(2 * first, 4)
        s = nt(flat(kv[c, 0, 0:2]), flat(far_qg[c, 0, rows])) * (SCALE * LOG2E)
        g = nt(flat(kv[c, 1, 0:2]), flat(far_qg[c, 1, rows]))
        cols = slice(first * HEAD_DIM, (first + 2) * HEAD_DIM)
        score[c, :, cols] = s
        gradw[c, :, cols] = g
        top = jnp.max(s, axis=0, keepdims=True)
        e = jnp.exp2(s - top)
        total = jnp.sum(e, axis=0, keepdims=True)
        delta = jnp.sum(e * g, axis=0, keepdims=True)
        for i in range(2):
            at = slice(i * HEAD_DIM, (i + 1) * HEAD_DIM)
            st_out[c, first + i, 0:1] = top[:, at]
            st_out[c, first + i, 1:2] = total[:, at]
            st_out[c, first + i, 2:3] = delta[:, at]

    def send_stats(c, first):
        for i in (first, first + 1):
            @pl.when(there[i])
            def _():
                stats(i, c).start()

    def stage(k, at, body):
        c = k - at

        @pl.when((c >= 0) & (c < heads))
        def _():
            body(c)

    def near(c):
        for d in range(2):
            @pl.when(there[d])
            def _():
                push(d, c).wait_recv()
        if RELAY_AT == NEAR_AT:
            send_on(c)
        meet(c, 0)
        send_stats(c, 0)

    def send_on(c):
        for d in range(2):
            @pl.when(middle)
            def _():
                start(relay, 1, d, c, far_qg.at[c, :, pl.ds(2 * d, 2)], relay_s.at[d, c])

    def local(c):
        @pl.when(c == 0)
        def _():
            for e in range(2):
                @pl.when(face_there[e])
                def _():
                    face_got(e).wait_recv()

        s = nt(flat(kv[c, 0]), flat(qg[c, 0])) * (SCALE * LOG2E)
        g = nt(flat(kv[c, 1]), flat(qg[c, 1]))
        row = lax.broadcasted_iota(jnp.int32, s.shape, 0)
        upper_from = jnp.where(has_upper, 128, 192)
        lower_to = jnp.where(has_lower, 256, 192)
        usable = (row < 128) | ((row >= upper_from) & (row < lower_to))
        s = jnp.where(usable, s, -FAR)
        score0[c] = s
        gradw0[c] = g
        top = jnp.max(s, axis=0, keepdims=True)
        e = jnp.exp2(s - top)
        st_own[c, 0:1] = top
        st_own[c, 1:2] = jnp.sum(e, axis=0, keepdims=True)
        st_own[c, 2:3] = jnp.sum(e * g, axis=0, keepdims=True)

    def far(c):
        @pl.when(c == 0)
        def _():
            pl.semaphore_wait(ready, sum(ok.astype(jnp.int32) for ok in there[:2]))

        for d in range(2):
            @pl.when(there[2 + d])
            def _():
                relay(d, c).wait_recv()
        meet(c, 2)
        send_stats(c, 2)

    def merge(c):
        for i in range(4):
            @pl.when(there[i])
            def _():
                stats_got(i, c).wait_recv()
        off = []
        for i in range(4):
            chosen = ((picks[c, 0] == SLOTS[i]) | (picks[c, 1] == SLOTS[i])) & there[i]
            off.append(jnp.where(chosen, 0.0, FAR).astype(jnp.float32))
        tops = [st_own[c, 0:1]] + [st_in[c, i, 0:1] - off[i] for i in range(4)]
        totals = [st_own[c, 1:2]] + [st_in[c, i, 1:2] for i in range(4)]
        deltas = [st_own[c, 2:3]] + [st_in[c, i, 2:3] for i in range(4)]
        top = functools.reduce(jnp.maximum, tops)
        shares = [jnp.exp2(x - top) for x in tops]
        total = functools.reduce(jnp.add, [x * y for x, y in zip(totals, shares)])
        delta = functools.reduce(jnp.add, [x * y for x, y in zip(deltas, shares)]) / total
        lse = top + jnp.log(total) * LOG2E
        for i in range(4):
            re_out[c, i, 0:1] = lse + off[i]
            re_out[c, i, 1:2] = delta
        for i in range(4):
            @pl.when(there[i])
            def _():
                ret(i, c).start()
        w = jnp.exp2(score0[c] - lse)
        ds = (w * (gradw0[c] - delta) * SCALE).astype(jnp.bfloat16)
        value_part = nn(w.astype(jnp.bfloat16), flat(qg[c, 1]))
        key_part = nn(ds, flat(qg[c, 0]))
        dq_own[c] = tn(ds, flat(kv[c, 0]))
        acc[c, 0] = key_part[:128]
        acc[c, 1] = value_part[:128]
        for e in range(2):
            at = slice(128 + 64 * e, 192 + 64 * e)
            face_out[c, e, 0] = key_part[at].astype(jnp.bfloat16)
            face_out[c, e, 1] = value_part[at].astype(jnp.bfloat16)
        for e in range(2):
            @pl.when(face_there[e])
            def _():
                face_back(e, c).start()

    def grad(c):
        for i in range(4):
            @pl.when(there[i])
            def _():
                ret_got(i, c).wait_recv()
        ws, dss = [], []
        for i in range(4):
            at = slice(i * HEAD_DIM, (i + 1) * HEAD_DIM)
            w = jnp.exp2(score[c, :, at] - re_in[c, i, 0:1])
            ws.append(w.astype(jnp.bfloat16))
            dss.append((w * (gradw[c, :, at] - re_in[c, i, 1:2]) * SCALE).astype(jnp.bfloat16))
        w, ds = jnp.concatenate(ws, axis=1), jnp.concatenate(dss, axis=1)
        dq = tn(ds, flat(kv[c, 0, 0:2]))
        d1_part[c, 1] = dq[0:128]
        d1_part[c, 0] = dq[128:256]
        d2_out[c, 1] = dq[256:384].astype(jnp.bfloat16)
        d2_out[c, 0] = dq[384:512].astype(jnp.bfloat16)
        for d in range(2):
            @pl.when(there[3 - d])
            def _():
                start(dq2, 2, d, c, d2_out.at[c, d], d2_s.at[d, c])
        acc[c, 0] += nn(ds, flat(far_qg[c, 0]))
        acc[c, 1] += nn(w, flat(far_qg[c, 1]))

    def pass_on(c):
        for d in range(2):
            @pl.when(middle)
            def _():
                dq2(d, c).wait_recv()
            d1_out[c, d] = (d1_part[c, d] + d2_in[c, d].astype(jnp.float32)).astype(jnp.bfloat16)

            @pl.when(there[1 - d])
            def _():
                start(dq1, 3, d, c, d1_out.at[c, d], d1_s.at[d, c])

    def store(o, c):
        cols = pl.ds(pl.multiple_of(c * HEAD_DIM, HEAD_DIM), HEAD_DIM)
        return pltpu.make_async_copy(
            result.at[c, o], (dq_out, dk_out, dv_out)[o].at[0, :, :, cols], out_sem.at[o, c]
        )

    def sent(c):
        for d in range(2):
            @pl.when(there[1 - d])
            def _():
                push(d, c).wait_send()

            @pl.when(middle)
            def _():
                relay(d, c).wait_send()

            @pl.when(there[3 - d])
            def _():
                dq2(d, c).wait_send()

            @pl.when(face_there[d])
            def _():
                face_back(d, c).wait_send()
        for i in range(4):
            @pl.when(there[i])
            def _():
                stats(i, c).wait_send()
                ret(i, c).wait_send()

    def end(c):
        sent(c)
        for e in range(2):
            @pl.when(face_there[e])
            def _():
                face_back_got(e, c).wait_recv()
        for which in range(2):
            for e in range(2):
                part = acc[c, which, pl.ds(64 * e, 64)] + face_in[c, e, which].astype(jnp.float32)
                result[c, 1 + which, e] = part.astype(jnp.bfloat16)
            store(1 + which, c).start()
        for d in range(2):
            @pl.when(there[d])
            def _():
                dq1(d, c).wait_recv()
        dq = dq_own[c] + d1_in[c, 0].astype(jnp.float32) + d1_in[c, 1].astype(jnp.float32)
        result[c, 0] = dq.astype(jnp.bfloat16).reshape(2, 64, HEAD_DIM)
        store(0, c).start()

    def on(kind, d):
        def body(c):
            @pl.when((t == ways[d]) & (lax.rem(c, 2) == 1))
            def _():
                if kind == 0 and d == 1:
                    @pl.when(c == 1)
                    def _():
                        pl.semaphore_wait(late, 1)
                forward_got(kind, c).wait_recv()
                forward(kind, d, c).start()

        return body

    def tick(k, carry):
        firsts = (NEAR_AT, ON_AT, PASS_AT - 1, END_AT - 1), (NEAR_AT, FAR_AT - 1, PASS_AT - 1, END_AT - 1)
        for kind in range(WAY_KINDS):
            stage(k, firsts[0][kind], on(kind, 0))
            stage(k, firsts[1][kind] + LATER, on(kind, 1))
        stage(k, NEAR_AT, near)

        @pl.when(k == FACES_AT)
        def _():
            start_faces(yields)

        if RELAY_AT != NEAR_AT:
            stage(k, RELAY_AT, send_on)
        stage(k, LOCAL_AT, local)
        stage(k, FAR_AT, far)
        stage(k, MERGE_AT, merge)
        stage(k, GRAD_AT, grad)
        stage(k, PASS_AT, pass_on)
        stage(k, END_AT, end)
        return carry

    lax.fori_loop(0, heads + END_AT + LATER, tick, 0)

    @each_head
    def _(c):
        for o in range(3):
            store(o, c).wait()
        for d in range(2):
            @pl.when(there[1 - d])
            def _():
                dq1(d, c).wait_send()

    @each_head
    def _(c):
        @pl.when(way & (lax.rem(c, 2) == 1))
        def _():
            for kind in range(WAY_KINDS):
                forward(kind, 0, c).wait_send()

    for e in range(2):
        @pl.when(face_there[e])
        def _():
            face_push(e).wait_send()


def solution(mesh):
    tiles_t, tiles_h = mesh.shape["tm"], mesh.shape["height"]

    def per_device(query_tok, key_tok, value_tok, grad_out, far_picks):
        heads = query_tok.shape[3] // HEAD_DIM
        shape = query_tok.shape
        tile = HEAD_DIM
        bf, f32 = jnp.bfloat16, jnp.float32
        dma = pltpu.SemaphoreType.DMA
        any_spec = pl.BlockSpec(memory_space=pl.ANY)
        return pl.pallas_call(
            functools.partial(kernel, (tiles_t, tiles_h, heads)),
            out_shape=[jax.ShapeDtypeStruct(shape, bf)] * 3,
            in_specs=[pl.BlockSpec(memory_space=pltpu.SMEM)] + [any_spec] * 4,
            out_specs=[any_spec] * 3,
            scratch_shapes=[
                pltpu.VMEM((heads, 2, 2, 64, HEAD_DIM), bf),
                pltpu.VMEM((heads, 2, 4, 64, HEAD_DIM), bf),
                pltpu.VMEM((heads, 2, 8, 64, HEAD_DIM), bf),
                pltpu.VMEM((heads, tile, 4 * tile), f32),
                pltpu.VMEM((heads, tile, 4 * tile), f32),
                pltpu.VMEM((heads, 2 * tile, tile), f32),
                pltpu.VMEM((heads, 2 * tile, tile), f32),
                pltpu.VMEM((heads, 4, 8, tile), f32),
                pltpu.VMEM((heads, 4, 8, tile), f32),
                pltpu.VMEM((heads, 8, tile), f32),
                pltpu.VMEM((heads, 4, 8, tile), f32),
                pltpu.VMEM((heads, 4, 8, tile), f32),
                pltpu.VMEM((heads, 2, tile, HEAD_DIM), bf),
                pltpu.VMEM((heads, 2, tile, HEAD_DIM), bf),
                pltpu.VMEM((heads, 2, tile, HEAD_DIM), f32),
                pltpu.VMEM((heads, 2, tile, HEAD_DIM), bf),
                pltpu.VMEM((heads, 2, tile, HEAD_DIM), bf),
                pltpu.VMEM((heads, tile, HEAD_DIM), f32),
                pltpu.VMEM((heads, 2, tile, HEAD_DIM), f32),
                pltpu.VMEM((heads, 2, 2, 64, HEAD_DIM), bf),
                pltpu.VMEM((heads, 2, 2, 64, HEAD_DIM), bf),
                pltpu.VMEM((heads // 2, 2, 2, 2, 64, HEAD_DIM), bf),
                pltpu.VMEM((heads // 2, 2, tile, HEAD_DIM), bf),
                pltpu.VMEM((heads, 3, 2, 64, HEAD_DIM), bf),
                dma((4, heads)),
                dma((2, heads)), dma((2, heads)),
                dma((2, heads)), dma((2, heads)),
                dma((4, heads)), dma((4, heads)),
                dma((4, heads)), dma((4, heads)),
                dma((2, heads)), dma((2, heads)),
                dma((2, heads)), dma((2, heads)),
                dma((2,)), dma((2,)),
                dma((2, heads)), dma((2, heads)),
                dma((4, heads // 2)), dma((4, heads // 2)),
                pltpu.SemaphoreType.REGULAR, pltpu.SemaphoreType.REGULAR,
                dma((3, heads)),
            ],
            compiler_params=pltpu.CompilerParams(
                collective_id=0, has_side_effects=True, vmem_limit_bytes=56 * 2**20
            ),
            name="tile_attention_grads",
        )(far_picks[0, 0], query_tok, key_tok, value_tok, grad_out)

    spec = P("tm", "height", None, None)
    return jax.shard_map(
        per_device, mesh=mesh, in_specs=(spec,) * 5, out_specs=(spec,) * 3, check_vma=False
    )
```
